256 devices in a mesh: stn: 64 (over z, y, core), band: 4 (over x).
Axes of the slice: x: 4, y: 4, z: 8, core: 2. Of those that a mesh axis runs over, the one named last changes fastest.
Arguments:
- voltages: bfloat16 [2, 512, 1024, 256], P(None, 'band', 'stn'), may hold values from -8 to 8
- group_count: int32 [4, 64], replicated, may hold values from 1 to 4, 128 in all within a row
- levels: int32 [4, 128], replicated, may hold values from 0 to 63
- bandpass: float32 [64], replicated, may hold values from 0.25 to 4
- block_order: int32 [64], replicated, may hold values from 0 to 63, each once
Outputs:
- tile_vis: bfloat16 [64, 64, 4, 2, 128, 128], P('stn', None, None, None, 'band')
The draws below stay inside these ranges and needn't reach their ends.
Inputs may be any that keep to these rules, and one draw needn't show every extreme that they name: `group_count`: in each band's row the 64 group sizes sum to 128, and the largest is exactly 4. `block_order`: each baseline block stands in exactly one slot.
All inputs are finite; a program needn't handle non-finite values.
Results may differ from the reference program's by a relative error of at most 0.001.
Values may be sent and summed in bfloat16 or wider, within the bound.
No kernel may reach another device: no remote copies, remote signals or barrier semaphores. Data moves between devices by JAX's collectives and lax.ppermute only.
A program may use at most 64 MiB of HBM per device.

```python
import math
import jax
import jax.numpy as jnp
import numpy as np
from jax import lax

SP = 1024
TIME = 256
BB = 128
LEVELS = 64
MOST = 4
GROUPS = 64
BANDS = 4
CH_BAND = 128
CHANNELS = 512
BLOCKS = 64


def draw_voltages(key, part):
    keys = jax.random.split(key, 4)
    shape = (2, CHANNELS, SP, TIME)
    noise = jax.random.normal(keys[0], shape, jnp.float32)
    amplitude = jax.random.uniform(keys[2], (1, SP, 1), jnp.float32, 0.5, 1.5)
    sky = jax.random.normal(keys[1], (2, CHANNELS, 1, TIME), jnp.float32)
    phase = jax.random.uniform(keys[3], (CHANNELS, SP, 1), jnp.float32, -math.pi, math.pi)
    cosine = jnp.cos(phase) * amplitude
    sine = jnp.sin(phase) * amplitude
    real_part = cosine * sky[0] - sine * sky[1] + noise[0]
    imag_part = sine * sky[0] + cosine * sky[1] + noise[1]
    return jnp.clip(jnp.stack([real_part, imag_part]), -8.0, 8.0).astype(jnp.bfloat16)


def plant(values, stream_key, low, top_value):
    dims = values.shape
    place = [jax.random.randint(jax.random.fold_in(stream_key, axis), (), 0, dims[axis]) for axis in range(len(dims))]
    values = values.at[tuple(place)].set(low)
    longest = dims.index(max(dims))
    place[longest] = (place[longest] + 1) % dims[longest]
    return values.at[tuple(place)].set(top_value)


def length_profile(count, total, reach, lean):
    loads = [(1 << 20) // math.isqrt(grade ** lean) + 1 for grade in range(2, count + 1)]
    rest, given = total - reach - (count - 1), [1] * (count - 1)
    while rest > 0:
        candidates = [i for i in range(count - 1) if given[i] < reach]
        mass, remaining = sum([loads[i] for i in candidates]), rest
        for i in candidates:
            addition = min(reach - given[i], max(1, remaining * loads[i] // mass), rest)
            given[i] = given[i] + addition
            rest = rest - addition
    return np.array([reach] + given)


def ragged(rng, count, total, limit, lean):
    if count == 2:
        one = jax.random.randint(rng, (), max(1, total - limit), min(limit, total - 1) + 1)
        return jnp.stack([one, total - one])
    lengths = jnp.asarray(length_profile(count, total, limit, lean), jnp.int32)
    twos = (count - 1) // 2
    source_of, taker = lengths[1:1 + 2 * twos:2], lengths[2:2 + 2 * twos:2]
    margin = jnp.minimum(source_of - 1, limit - taker)
    moved = jax.random.randint(jax.random.fold_in(rng, 1), (twos,), 0, 1 << 20) % (margin + 1)
    lengths = lengths.at[1:1 + 2 * twos:2].set(source_of - moved).at[2:2 + 2 * twos:2].set(taker + moved)
    return lengths[jax.random.permutation(jax.random.fold_in(rng, 2), count)]


def setup_inputs(seed: int = 0) -> dict:
    splits = jax.random.split(jax.random.key(seed), 6)
    return {
        "voltages": draw_voltages(jax.random.fold_in(splits[5], 71), 0),
        "group_count": jax.vmap(lambda own: ragged(own, GROUPS, CH_BAND, MOST, 2))(jax.random.split(splits[1], BANDS)).reshape((BANDS, GROUPS)).astype(jnp.int32),
        "levels": plant(jax.random.randint(splits[2], (BANDS, CH_BAND), 0, LEVELS), jax.random.fold_in(splits[2], 1), 0, LEVELS - 1).astype(jnp.int32),
        "bandpass": jnp.clip(jnp.exp(jax.random.uniform(splits[3], (LEVELS,), jnp.float32, math.log(0.25), math.log(4.0))), 0.25, 4.0),
        "block_order": jax.random.permutation(splits[4], BLOCKS).astype(jnp.int32),
    }


def correlate_channel(channel):
    real_part = channel[0].astype(jnp.float32)
    imag_part = channel[1].astype(jnp.float32)
    right_side = jnp.concatenate([real_part, imag_part], axis=1)
    swapped = jnp.concatenate([imag_part, -real_part], axis=1)
    stacked = jnp.concatenate([right_side, swapped], axis=0)
    return lax.dot_general(stacked, right_side, (((1,), (1,)), ((), ())), precision=lax.Precision.HIGHEST)


def reference(voltages, group_count, levels, bandpass, block_order):
    block_count = SP // BB
    per_band = []
    for band_index in range(BANDS):
        counts = group_count[band_index].astype(jnp.int32)
        starts = (jnp.cumsum(counts) - counts).astype(jnp.int32)
        gain_row = bandpass[levels[band_index]]
        band_volts = voltages[:, band_index * CH_BAND:(band_index + 1) * CH_BAND]

        def one_group(group_pair, band_volts=band_volts, gain_row=gain_row):
            group_start, group_size = group_pair
            divisor = group_size.astype(jnp.float32) * TIME

            def accumulate(slot, totals):
                chan_index = (group_start + slot).astype(jnp.int32)
                channel = lax.dynamic_index_in_dim(band_volts, chan_index, 1, keepdims=False)
                weight = lax.dynamic_index_in_dim(gain_row, chan_index, 0, keepdims=False) / divisor
                return totals + weight * correlate_channel(channel)

            totals = lax.fori_loop(jnp.int32(0), group_size, accumulate, jnp.zeros((2 * SP, SP), jnp.float32))
            return totals.astype(jnp.bfloat16)

        per_band.append(lax.map(one_group, (starts, counts)))
    visibility = jnp.stack(per_band, axis=1)
    visibility = visibility.reshape(GROUPS, BANDS, 2, block_count, BB, block_count, BB)
    blocks = visibility.transpose(3, 5, 0, 1, 2, 4, 6).reshape(BLOCKS, GROUPS, BANDS, 2, BB, BB)
    return jnp.take(blocks, block_order, axis=0)
```

```python
import functools

import jax
import jax.numpy as jnp
from jax import lax
from jax.experimental import pallas as pl
from jax.experimental.pallas import tpu as pltpu
from jax.sharding import PartitionSpec as P

SP = 1024
TIME = 256
BB = 128
MOST = 4
GROUPS = 64
BANDS = 4
HALF = GROUPS // 2
CHIPS = 32
SLOTS = MOST + 1
SIDE = SP // BB
SUPER = 256
ROWS = BB // BANDS

SMEM = pl.BlockSpec(memory_space=pltpu.SMEM)
VMEM = pl.BlockSpec(memory_space=pltpu.VMEM)


def first_places(count_ref, band):
    def tally(g, held):
        size = count_ref[band, g]
        return tuple(n + (size == s).astype(jnp.int32) for n, s in zip(held, (4, 3, 2)))

    zero = jnp.int32(0)
    fours, threes, twos = lax.fori_loop(0, GROUPS, tally, (zero, zero, zero), unroll=8)
    return zero, fours, fours + threes, fours + threes + twos


def next_place(places, size):
    at = [size == s for s in (4, 3, 2, 1)]
    place = jnp.where(at[0], places[0], jnp.where(at[1], places[1], jnp.where(at[2], places[2], places[3])))
    return place, tuple(p + a.astype(jnp.int32) for p, a in zip(places, at))


def build_kernel(count_ref, volt_ref, send_ref):
    band = lax.axis_index("band")

    def one_group(g, held):
        places, start = held
        size = count_ref[band, g]
        place, places = next_place(places, size)
        large = place < HALF
        chip = jnp.where(large, place, GROUPS - 1 - place)
        base = jnp.where(large, SLOTS - size, 0)

        def one_channel(i, carry):
            for part in range(2):
                send_ref[2 * chip + part, base + i] = volt_ref[part, start + i]
            return carry

        lax.fori_loop(0, size, one_channel, 0)
        return places, start + size

    lax.fori_loop(0, GROUPS, one_group, (first_places(count_ref, band), jnp.int32(0)))


def index_kernel(count_ref, level_ref, gain_ref, order_ref, meta_ref, weight_ref, slot_ref, place_ref):
    mine = lax.axis_index("stn")
    my_band = lax.axis_index("band")
    chip = mine // 2
    meta_ref[4] = lax.rem(mine, 2)

    def one_band(band, carry):
        def one_group(g, held):
            places, start = held
            size = count_ref[band, g]
            place, places = next_place(places, size)
            place_ref[band, g] = place
            own = (band == my_band) & ((place == chip) | (place == GROUPS - 1 - chip))

            @pl.when(own)
            def _():
                large = (place < HALF).astype(jnp.int32)
                meta_ref[large] = size
                base = jnp.where(large == 1, SLOTS - size, 0)
                scale = jnp.where(
                    size == 4,
                    1.0 / (4 * TIME),
                    jnp.where(size == 3, 1.0 / (3 * TIME), jnp.where(size == 2, 1.0 / (2 * TIME), 1.0 / TIME)),
                )

                def one_channel(i, carry):
                    weight_ref[base + i] = gain_ref[level_ref[band, start + i]] * scale
                    return carry

                lax.fori_loop(0, size, one_channel, 0)

            return places, start + size

        lax.fori_loop(0, GROUPS, one_group, (first_places(count_ref, band), jnp.int32(0)))
        return carry

    lax.fori_loop(0, BANDS, one_band, 0)

    def one_slot(s, carry):
        slot_ref[order_ref[s]] = s
        return carry

    lax.fori_loop(0, GROUPS, one_slot, 0, unroll=8)


def visibility_kernel(meta_ref, weight_ref, slot_ref, mine_ref, other_ref, out_ref, left, right, total):
    core = meta_ref[4]
    sign = (1 - 2 * core).astype(jnp.float32)

    for large in range(2):
        size = meta_ref[large]
        base = SLOTS - size if large else 0

        def one_channel(i, carry):
            t = base + i
            weight = weight_ref[t]
            u = mine_ref[:, t].reshape(SP, TIME)
            v = other_ref[:, t].reshape(SP, TIME)
            left[:, :TIME] = u

            @pl.when(core == 0)
            def _():
                left[:, TIME:] = v
                right[:, :TIME] = u
                right[:, TIME:] = v

            @pl.when(core == 1)
            def _():
                left[:, TIME:] = -v
                right[:, :TIME] = v
                right[:, TIME:] = u

            def products(first):
                for row in range(0, SP, SUPER):
                    part = weight * lax.dot_general(
                        left[row : row + SUPER],
                        right[row:],
                        (((1,), (1,)), ((), ())),
                        preferred_element_type=jnp.float32,
                    )
                    if first:
                        total[row : row + SUPER, row:] = part
                    else:
                        total[row : row + SUPER, row:] += part

            @pl.when(i == 0)
            def _():
                products(True)

            @pl.when(i > 0)
            def _():
                products(False)

            return carry

        lax.fori_loop(0, size, one_channel, 0)

        def store(p, q, block):
            out_ref[slot_ref[SIDE * p + q], :, large] = block.astype(jnp.bfloat16).reshape(BANDS, ROWS, BB)

        per = SUPER // BB
        for p in range(SIDE):
            for q in range(p // per * per, SIDE):
                block = total[p * BB : (p + 1) * BB, q * BB : (q + 1) * BB]
                store(p, q, block)
                if q // per > p // per:
                    store(q, p, sign * block.T)


def place_kernel(place_ref, got_ref, out_ref):
    step = pl.program_id(0)
    per = out_ref.shape[0]

    def one_group(i, carry):
        for band in range(BANDS):
            place = place_ref[band, step * per + i]
            large = (place < HALF).astype(jnp.int32)
            chip = jnp.where(place < HALF, place, GROUPS - 1 - place)
            out_ref[i, band] = got_ref[chip, :, band, large]
        return carry

    lax.fori_loop(0, per, one_group, 0)


def body(voltages, group_count, levels, bandpass, block_order):
    stations, samples = voltages.shape[2], voltages.shape[3]
    owners = lax.axis_size("stn")
    sending = pl.pallas_call(
        build_kernel,
        out_shape=jax.ShapeDtypeStruct((owners, SLOTS, stations, samples), jnp.bfloat16),
        in_specs=[SMEM, VMEM],
        out_specs=VMEM,
        cost_estimate=pl.CostEstimate(flops=0, bytes_accessed=5 << 20, transcendentals=0),
        name="build",
    )(group_count, voltages)
    meta, weights, slots, places = pl.pallas_call(
        index_kernel,
        out_shape=(
            jax.ShapeDtypeStruct((8,), jnp.int32),
            jax.ShapeDtypeStruct((8,), jnp.float32),
            jax.ShapeDtypeStruct((GROUPS,), jnp.int32),
            jax.ShapeDtypeStruct((BANDS, GROUPS), jnp.int32),
        ),
        in_specs=[SMEM] * 4,
        out_specs=(SMEM,) * 4,
        cost_estimate=pl.CostEstimate(flops=0, bytes_accessed=8 << 20, transcendentals=0),
        name="index",
    )(group_count, levels, bandpass, block_order)
    mine = lax.all_to_all(sending, "stn", split_axis=0, concat_axis=0, tiled=True)
    other = lax.ppermute(mine, "stn", [(i, i ^ 1) for i in range(owners)])
    blocks = pl.pallas_call(
        visibility_kernel,
        out_shape=jax.ShapeDtypeStruct((GROUPS, BANDS, 2, ROWS, BB), jnp.bfloat16),
        in_specs=[SMEM, SMEM, SMEM, VMEM, VMEM],
        out_specs=VMEM,
        scratch_shapes=[
            pltpu.VMEM((SP, 2 * TIME), jnp.bfloat16),
            pltpu.VMEM((SP, 2 * TIME), jnp.bfloat16),
            pltpu.VMEM((SP, SP), jnp.float32),
        ],
        cost_estimate=pl.CostEstimate(flops=4 << 30, bytes_accessed=9 << 20, transcendentals=0),
        name="visibility",
    )(meta, weights, slots, mine, other)
    blocks = blocks.reshape(GROUPS * BANDS, 2, ROWS, BB)
    got = lax.all_to_all(blocks, ("stn", "band"), split_axis=0, concat_axis=0, tiled=True)
    got = got.reshape(CHIPS, 2, BANDS, 2, ROWS, BB)
    steps = 8
    out = pl.pallas_call(
        place_kernel,
        grid=(steps,),
        out_shape=jax.ShapeDtypeStruct((GROUPS, BANDS, 2, ROWS, BB), jnp.bfloat16),
        in_specs=[SMEM, VMEM],
        out_specs=pl.BlockSpec((GROUPS // steps, BANDS, 2, ROWS, BB), lambda i: (i, 0, 0, 0, 0)),
        cost_estimate=pl.CostEstimate(flops=0, bytes_accessed=8 << 20, transcendentals=0),
        name="place",
    )(places, got)
    return out.reshape(1, GROUPS, BANDS, 2, ROWS, BB)


def solution(mesh):
    return jax.shard_map(
        body,
        mesh=mesh,
        in_specs=(P(None, "band", "stn", None), P(), P(), P(), P()),
        out_specs=P("stn", None, None, None, "band", None),
        check_vma=False,
    )
```

```python
import jax
import jax.numpy as jnp
from jax import lax
from jax.experimental import pallas as pl
from jax.experimental.pallas import tpu as pltpu
from jax.sharding import PartitionSpec as P


SP = 1024
TIME = 256
BB = 128
MOST = 4
GROUPS = 64
BANDS = 4
HALF = GROUPS // 2
CHIPS = 32
SLOTS = MOST + 1
SIDE = SP // BB
SUPER = 256
ROWS = BB // BANDS

SMEM = pl.BlockSpec(memory_space=pltpu.SMEM)
VMEM = pl.BlockSpec(memory_space=pltpu.VMEM)
ANY = pl.BlockSpec(memory_space=pl.ANY)


def first_places(count_ref, band):
    def tally(g, held):
        size = count_ref[band, g]
        return tuple(n + (size == s).astype(jnp.int32) for n, s in zip(held, (4, 3, 2)))

    zero = jnp.int32(0)
    fours, threes, twos = lax.fori_loop(0, GROUPS, tally, (zero, zero, zero), unroll=8)
    return zero, fours, fours + threes, fours + threes + twos


def next_place(places, size):
    at = [size == s for s in (4, 3, 2, 1)]
    place = jnp.where(at[0], places[0], jnp.where(at[1], places[1], jnp.where(at[2], places[2], places[3])))
    return place, tuple(p + a.astype(jnp.int32) for p, a in zip(places, at))


def build_kernel(count_ref, volt_ref, send_ref, held, arrival):
    band = lax.axis_index("band")
    copy = pltpu.make_async_copy(volt_ref, held, arrival)
    copy.start()
    places = first_places(count_ref, band)
    copy.wait()

    def one_group(g, carry):
        places, start = carry
        size = count_ref[band, g]
        place, places = next_place(places, size)
        large = place < HALF
        chip = jnp.where(large, place, GROUPS - 1 - place)
        base = jnp.where(large, SLOTS - size, 0)
        for i in range(MOST):
            step = jnp.minimum(i, size - 1)
            for part in range(2):
                send_ref[2 * chip + part, base + step] = held[part, start + step]
        return places, start + size

    lax.fori_loop(0, GROUPS, one_group, (places, jnp.int32(0)), unroll=4)


def index_kernel(count_ref, level_ref, gain_ref, order_ref, meta_ref, weight_ref, slot_ref, place_ref):
    mine = lax.axis_index("stn")
    my_band = lax.axis_index("band")
    chip = mine // 2
    meta_ref[4] = lax.rem(mine, 2)

    def one_band(band, carry):
        def one_group(g, held):
            places, start = held
            size = count_ref[band, g]
            place, places = next_place(places, size)
            place_ref[band, g] = place
            own = (band == my_band) & ((place == chip) | (place == GROUPS - 1 - chip))

            @pl.when(own)
            def _():
                large = (place < HALF).astype(jnp.int32)
                meta_ref[large] = size
                base = jnp.where(large == 1, SLOTS - size, 0)
                scale = jnp.where(
                    size == 4,
                    1.0 / (4 * TIME),
                    jnp.where(size == 3, 1.0 / (3 * TIME), jnp.where(size == 2, 1.0 / (2 * TIME), 1.0 / TIME)),
                )

                def one_channel(i, carry):
                    weight_ref[base + i] = gain_ref[level_ref[band, start + i]] * scale
                    return carry

                lax.fori_loop(0, size, one_channel, 0)

            return places, start + size

        lax.fori_loop(0, GROUPS, one_group, (first_places(count_ref, band), jnp.int32(0)))
        return carry

    lax.fori_loop(0, BANDS, one_band, 0)

    def one_slot(s, carry):
        slot_ref[order_ref[s]] = s
        return carry

    lax.fori_loop(0, GROUPS, one_slot, 0, unroll=8)


def visibility_kernel(meta_ref, weight_ref, slot_ref, mine_ref, other_ref, out_ref, total):
    core = meta_ref[4]
    sign = (1 - 2 * core).astype(jnp.float32)
    stations = mine_ref.shape[2]
    tall = SUPER // stations

    for large in range(2):
        size = meta_ref[large]
        base = SLOTS - size if large else 0

        def one_channel(i, carry):
            t = base + i
            weight = weight_ref[t]

            def products(first, imaginary):
                for row in range(0, SP, SUPER):
                    r = row // stations
                    u = mine_ref[r : r + tall, t].reshape(SUPER, TIME)
                    v = other_ref[r : r + tall, t].reshape(SUPER, TIME)
                    all_u = mine_ref[r:, t].reshape(SP - row, TIME)
                    all_v = other_ref[r:, t].reshape(SP - row, TIME)
                    if imaginary:
                        left, right = (u, -v), (all_v, all_u)
                    else:
                        left, right = (u, v), (all_u, all_v)
                    part = weight * lax.dot_general(
                        jnp.concatenate(left, 1),
                        jnp.concatenate(right, 1),
                        (((1,), (1,)), ((), ())),
                        preferred_element_type=jnp.float32,
                    )
                    if first:
                        total[row : row + SUPER, row:] = part
                    else:
                        total[row : row + SUPER, row:] += part

            for imaginary in range(2):

                @pl.when((core == imaginary) & (i == 0))
                def _():
                    products(True, imaginary)

                @pl.when((core == imaginary) & (i > 0))
                def _():
                    products(False, imaginary)

            return carry

        lax.fori_loop(0, size, one_channel, 0)

        def store(p, q, block):
            out_ref[slot_ref[SIDE * p + q], :, large] = block.astype(jnp.bfloat16).reshape(BANDS, ROWS, BB)

        per = SUPER // BB
        for p in range(SIDE):
            for q in range(p // per * per, SIDE):
                block = total[p * BB : (p + 1) * BB, q * BB : (q + 1) * BB]
                store(p, q, block)
                if q // per > p // per:
                    store(q, p, sign * block.T)


def place_kernel(place_ref, got_ref, out_ref, landed):
    for band in range(BANDS):

        def one_group(g, carry):
            place = place_ref[band, g]
            large = (place < HALF).astype(jnp.int32)
            chip = jnp.where(place < HALF, place, GROUPS - 1 - place)
            pltpu.make_async_copy(got_ref.at[chip, :, band, large], out_ref.at[g, band], landed).start()
            return carry

        lax.fori_loop(0, GROUPS, one_group, 0, unroll=8)
    pltpu.make_async_copy(out_ref, out_ref, landed).wait()


def body(voltages, group_count, levels, bandpass, block_order):
    stations, samples = voltages.shape[2], voltages.shape[3]
    owners = lax.axis_size("stn")
    sending = pl.pallas_call(
        build_kernel,
        out_shape=jax.ShapeDtypeStruct((owners, SLOTS, stations, samples), jnp.bfloat16),
        in_specs=[SMEM, ANY],
        out_specs=VMEM,
        scratch_shapes=[pltpu.VMEM(voltages.shape, voltages.dtype), pltpu.SemaphoreType.DMA],
        cost_estimate=pl.CostEstimate(flops=0, bytes_accessed=5 << 20, transcendentals=0),
        name="build",
    )(group_count, voltages)
    meta, weights, slots, places = pl.pallas_call(
        index_kernel,
        out_shape=(
            jax.ShapeDtypeStruct((8,), jnp.int32),
            jax.ShapeDtypeStruct((8,), jnp.float32),
            jax.ShapeDtypeStruct((GROUPS,), jnp.int32),
            jax.ShapeDtypeStruct((BANDS, GROUPS), jnp.int32),
        ),
        in_specs=[SMEM] * 4,
        out_specs=(SMEM,) * 4,
        cost_estimate=pl.CostEstimate(flops=0, bytes_accessed=8 << 20, transcendentals=0),
        compiler_params=pltpu.CompilerParams(vmem_limit_bytes=2 << 20),
        name="index",
    )(group_count, levels, bandpass, block_order)
    mine = lax.all_to_all(sending, "stn", split_axis=0, concat_axis=0, tiled=True)
    other = lax.ppermute(mine, "stn", [(i, i ^ 1) for i in range(owners)])
    blocks = pl.pallas_call(
        visibility_kernel,
        out_shape=jax.ShapeDtypeStruct((GROUPS, BANDS, 2, ROWS, BB), jnp.bfloat16),
        in_specs=[SMEM, SMEM, SMEM, VMEM, VMEM],
        out_specs=VMEM,
        scratch_shapes=[
            pltpu.VMEM((SP, SP), jnp.float32),
        ],
        cost_estimate=pl.CostEstimate(flops=4 << 30, bytes_accessed=9 << 20, transcendentals=0),
        compiler_params=pltpu.CompilerParams(vmem_limit_bytes=24 << 20),
        name="visibility",
    )(meta, weights, slots, mine, other)
    blocks = blocks.reshape(GROUPS * BANDS, 2, ROWS, BB)
    got = lax.all_to_all(blocks, ("stn", "band"), split_axis=0, concat_axis=0, tiled=True)
    got = got.reshape(CHIPS, 2, BANDS, 2, ROWS, BB)
    out = pl.pallas_call(
        place_kernel,
        out_shape=jax.ShapeDtypeStruct((GROUPS, BANDS, 2, ROWS, BB), jnp.bfloat16),
        in_specs=[SMEM, VMEM],
        out_specs=ANY,
        scratch_shapes=[pltpu.SemaphoreType.DMA],
        cost_estimate=pl.CostEstimate(flops=0, bytes_accessed=8 << 20, transcendentals=0),
        compiler_params=pltpu.CompilerParams(vmem_limit_bytes=8 << 20),
        name="place",
    )(places, got)
    return out.reshape(1, GROUPS, BANDS, 2, ROWS, BB)


def solution(mesh):
    return jax.shard_map(
        body,
        mesh=mesh,
        in_specs=(P(None, "band", "stn", None), P(), P(), P(), P()),
        out_specs=P("stn", None, None, None, "band", None),
        check_vma=False,
    )
```

```python
import functools

import jax
import jax.numpy as jnp
from jax import lax
from jax.experimental import pallas as pl
from jax.experimental.pallas import tpu as pltpu
from jax.sharding import PartitionSpec as P


SP = 1024
TIME = 256
BB = 128
MOST = 4
GROUPS = 64
BANDS = 4
HALF = GROUPS // 2
CHIPS = 32
SLOTS = MOST + 1
SIDE = SP // BB
SUPER = 256
ROWS = BB // BANDS

SMEM = pl.BlockSpec(memory_space=pltpu.SMEM)
VMEM = pl.BlockSpec(memory_space=pltpu.VMEM)
ANY = pl.BlockSpec(memory_space=pl.ANY)


def first_places(count_ref, band):
    def tally(g, held):
        size = count_ref[band, g]
        return tuple(n + (size >= s).astype(jnp.int32) for n, s in zip(held, (4, 3, 2)))

    zero = jnp.int32(0)
    return zero, *lax.fori_loop(0, GROUPS, tally, (zero, zero, zero), unroll=True)


def next_place(places, size):
    at = [size == s for s in (4, 3, 2, 1)]
    place = jnp.where(at[0], places[0], jnp.where(at[1], places[1], jnp.where(at[2], places[2], places[3])))
    return place, tuple(p + a.astype(jnp.int32) for p, a in zip(places, at))


def build_kernel(count_ref, volt_ref, send_ref, count, held, arrivals, sent):
    band = lax.axis_index("band")
    count_copy = pltpu.make_async_copy(count_ref, count, arrivals.at[0])
    volt_copy = pltpu.make_async_copy(volt_ref, held, arrivals.at[1])
    count_copy.start()
    volt_copy.start()
    count_copy.wait()
    places = first_places(count, band)
    volt_copy.wait()

    def one_group(g, carry):
        places, start = carry
        size = count[band, g]
        place, places = next_place(places, size)
        large = place < HALF
        chip = jnp.where(large, place, GROUPS - 1 - place)
        base = jnp.where(large, SLOTS - size, 0)

        def send(i):
            pltpu.make_async_copy(held.at[:, start + i], send_ref.at[pl.ds(2 * chip, 2), base + i], sent).start()

        send(0)
        for i in range(1, MOST):
            pl.when(i < size)(functools.partial(send, i))
        return places, start + size

    lax.fori_loop(0, GROUPS, one_group, (places, jnp.int32(0)), unroll=4)
    pltpu.make_async_copy(held, held, sent).wait()


def index_kernel(count_ref, level_ref, gain_ref, order_ref, meta_ref, weight_ref, slot_ref, place_ref):
    mine = lax.axis_index("stn")
    my_band = lax.axis_index("band")
    chip = mine // 2
    meta_ref[4] = lax.rem(mine, 2)

    def one_band(band, carry):
        def one_group(g, held):
            places, start = held
            size = count_ref[band, g]
            place, places = next_place(places, size)
            place_ref[band, g] = place
            own = (band == my_band) & ((place == chip) | (place == GROUPS - 1 - chip))

            @pl.when(own)
            def _():
                large = (place < HALF).astype(jnp.int32)
                meta_ref[large] = size
                base = jnp.where(large == 1, SLOTS - size, 0)
                scale = jnp.where(
                    size == 4,
                    1.0 / (4 * TIME),
                    jnp.where(size == 3, 1.0 / (3 * TIME), jnp.where(size == 2, 1.0 / (2 * TIME), 1.0 / TIME)),
                )

                def one_channel(i, carry):
                    weight_ref[base + i] = gain_ref[level_ref[band, start + i]] * scale
                    return carry

                lax.fori_loop(0, size, one_channel, 0)

            return places, start + size

        lax.fori_loop(0, GROUPS, one_group, (first_places(count_ref, band), jnp.int32(0)))
        return carry

    lax.fori_loop(0, BANDS, one_band, 0)

    def one_slot(s, carry):
        slot_ref[order_ref[s]] = s
        return carry

    lax.fori_loop(0, GROUPS, one_slot, 0, unroll=8)


def visibility_kernel(meta_ref, weight_ref, slot_ref, mine_ref, other_ref, out_ref, total):
    core = meta_ref[4]
    sign = (1 - 2 * core).astype(jnp.float32)
    stations = mine_ref.shape[2]
    tall = SUPER // stations

    for large in range(2):
        size = meta_ref[large]
        base = SLOTS - size if large else 0

        def one_channel(i, carry):
            t = base + i
            weight = weight_ref[t]

            def products(first, imaginary):
                for row in range(0, SP, SUPER):
                    r = row // stations
                    u = mine_ref[r : r + tall, t].reshape(SUPER, TIME)
                    v = other_ref[r : r + tall, t].reshape(SUPER, TIME)
                    all_u = mine_ref[r:, t].reshape(SP - row, TIME)
                    all_v = other_ref[r:, t].reshape(SP - row, TIME)
                    if imaginary:
                        left, right = (u, -v), (all_v, all_u)
                    else:
                        left, right = (u, v), (all_u, all_v)
                    part = weight * lax.dot_general(
                        jnp.concatenate(left, 1),
                        jnp.concatenate(right, 1),
                        (((1,), (1,)), ((), ())),
                        preferred_element_type=jnp.float32,
                    )
                    if first:
                        total[row : row + SUPER, row:] = part
                    else:
                        total[row : row + SUPER, row:] += part

            for imaginary in range(2):

                @pl.when((core == imaginary) & (i == 0))
                def _():
                    products(True, imaginary)

                @pl.when((core == imaginary) & (i > 0))
                def _():
                    products(False, imaginary)

            return carry

        lax.fori_loop(0, size, one_channel, 0)

        def store(p, q, block):
            out_ref[slot_ref[SIDE * p + q], :, large] = block.reshape(BANDS, ROWS, BB)

        per = SUPER // BB
        for p in range(SIDE):
            for q in range(p // per * per, SIDE):
                block = total[p * BB : (p + 1) * BB, q * BB : (q + 1) * BB]
                store(p, q, block.astype(jnp.bfloat16))
                if q // per > p // per:
                    store(q, p, (sign * block).astype(jnp.bfloat16).T)


def place_kernel(place_ref, got_ref, out_ref, landed):
    for band in range(BANDS):

        def one_group(g, carry):
            place = place_ref[band, g]
            large = (place < HALF).astype(jnp.int32)
            chip = jnp.where(place < HALF, place, GROUPS - 1 - place)
            pltpu.make_async_copy(got_ref.at[chip, :, band, large], out_ref.at[g, band], landed).start()
            return carry

        lax.fori_loop(0, GROUPS, one_group, 0, unroll=8)
    pltpu.make_async_copy(out_ref, out_ref, landed).wait()


def body(voltages, group_count, levels, bandpass, block_order):
    stations, samples = voltages.shape[2], voltages.shape[3]
    owners = lax.axis_size("stn")
    sending = pl.pallas_call(
        build_kernel,
        out_shape=jax.ShapeDtypeStruct((owners, SLOTS, stations, samples), jnp.bfloat16),
        in_specs=[ANY, ANY],
        out_specs=ANY,
        scratch_shapes=[
            pltpu.SMEM(group_count.shape, group_count.dtype),
            pltpu.VMEM(voltages.shape, voltages.dtype),
            pltpu.SemaphoreType.DMA((2,)),
            pltpu.SemaphoreType.DMA,
        ],
        cost_estimate=pl.CostEstimate(flops=0, bytes_accessed=5 << 20, transcendentals=0),
        name="build",
    )(group_count, voltages)
    meta, weights, slots, places = pl.pallas_call(
        index_kernel,
        out_shape=(
            jax.ShapeDtypeStruct((8,), jnp.int32),
            jax.ShapeDtypeStruct((8,), jnp.float32),
            jax.ShapeDtypeStruct((GROUPS,), jnp.int32),
            jax.ShapeDtypeStruct((BANDS, GROUPS), jnp.int32),
        ),
        in_specs=[SMEM] * 4,
        out_specs=(SMEM,) * 4,
        cost_estimate=pl.CostEstimate(flops=0, bytes_accessed=8 << 20, transcendentals=0),
        compiler_params=pltpu.CompilerParams(vmem_limit_bytes=2 << 20),
        name="index",
    )(group_count, levels, bandpass, block_order)
    mine = lax.all_to_all(sending, "stn", split_axis=0, concat_axis=0, tiled=True)
    other = lax.ppermute(mine, "stn", [(i, i ^ 1) for i in range(owners)])
    blocks = pl.pallas_call(
        visibility_kernel,
        out_shape=jax.ShapeDtypeStruct((GROUPS, BANDS, 2, ROWS, BB), jnp.bfloat16),
        in_specs=[SMEM, SMEM, SMEM, VMEM, VMEM],
        out_specs=VMEM,
        scratch_shapes=[
            pltpu.VMEM((SP, SP), jnp.float32),
        ],
        cost_estimate=pl.CostEstimate(flops=4 << 30, bytes_accessed=9 << 20, transcendentals=0),
        compiler_params=pltpu.CompilerParams(vmem_limit_bytes=24 << 20),
        name="visibility",
    )(meta, weights, slots, mine, other)
    blocks = blocks.reshape(GROUPS * BANDS, 2, ROWS, BB)
    got = lax.all_to_all(blocks, ("stn", "band"), split_axis=0, concat_axis=0, tiled=True)
    got = got.reshape(CHIPS, 2, BANDS, 2, ROWS, BB)
    out = pl.pallas_call(
        place_kernel,
        out_shape=jax.ShapeDtypeStruct((GROUPS, BANDS, 2, ROWS, BB), jnp.bfloat16),
        in_specs=[SMEM, VMEM],
        out_specs=ANY,
        scratch_shapes=[pltpu.SemaphoreType.DMA],
        cost_estimate=pl.CostEstimate(flops=0, bytes_accessed=8 << 20, transcendentals=0),
        compiler_params=pltpu.CompilerParams(vmem_limit_bytes=8 << 20),
        name="place",
    )(places, got)
    return out.reshape(1, GROUPS, BANDS, 2, ROWS, BB)


def solution(mesh):
    return jax.shard_map(
        body,
        mesh=mesh,
        in_specs=(P(None, "band", "stn", None), P(), P(), P(), P()),
        out_specs=P("stn", None, None, None, "band", None),
        check_vma=False,
    )
```

```python
import functools

import jax
import jax.numpy as jnp
from jax import lax
from jax.experimental import pallas as pl
from jax.experimental.pallas import tpu as pltpu
from jax.sharding import PartitionSpec as P


SP = 1024
TIME = 256
BB = 128
MOST = 4
GROUPS = 64
BANDS = 4
HALF = GROUPS // 2
CHIPS = 32
SLOTS = MOST + 1
SIDE = SP // BB
SUPER = 256
ROWS = BB // BANDS

SMEM = pl.BlockSpec(memory_space=pltpu.SMEM)
VMEM = pl.BlockSpec(memory_space=pltpu.VMEM)
ANY = pl.BlockSpec(memory_space=pl.ANY)


def first_places(count_ref, band):
    def tally(g, held):
        size = count_ref[band, g]
        return tuple(n + (size >= s).astype(jnp.int32) for n, s in zip(held, (4, 3, 2)))

    zero = jnp.int32(0)
    return zero, *lax.fori_loop(0, GROUPS, tally, (zero, zero, zero), unroll=True)


def next_place(places, size):
    at = [size == s for s in (4, 3, 2, 1)]
    place = jnp.where(at[0], places[0], jnp.where(at[1], places[1], jnp.where(at[2], places[2], places[3])))
    return place, tuple(p + a.astype(jnp.int32) for p, a in zip(places, at))


def build_kernel(count_ref, volt_ref, send_ref, count, held, arrivals, sent):
    band = lax.axis_index("band")
    count_copy = pltpu.make_async_copy(count_ref, count, arrivals.at[0])
    volt_copy = pltpu.make_async_copy(volt_ref, held, arrivals.at[1])
    count_copy.start()
    volt_copy.start()
    count_copy.wait()
    places = first_places(count, band)
    volt_copy.wait()

    def one_group(g, carry):
        places, start = carry
        size = count[band, g]
        place, places = next_place(places, size)
        large = place < HALF
        chip = jnp.where(large, place, GROUPS - 1 - place)
        base = jnp.where(large, SLOTS - size, 0)

        alone = jnp.where(large, size - 1, size)

        def send(i):
            slot = base + i
            target = send_ref.at[2 * chip + (slot >> 1), pl.ds(2 * (slot & 1), 2)]
            pltpu.make_async_copy(held.at[:, start + i], target, sent).start()

        for i in range(MOST - 1):
            pl.when(i < alone)(functools.partial(send, i))

        @pl.when(large)
        def _():
            target = send_ref.at[pl.ds(2 * chip, 2), SLOTS - 1]
            pltpu.make_async_copy(held.at[:, start + size - 1], target, sent).start()

        return places, start + size

    lax.fori_loop(0, GROUPS, one_group, (places, jnp.int32(0)), unroll=4)
    pltpu.make_async_copy(held, held, sent).wait()


def index_kernel(count_ref, level_ref, gain_ref, order_ref, meta_ref, weight_ref, slot_ref, place_ref):
    mine = lax.axis_index("stn")
    my_band = lax.axis_index("band")
    chip = mine // 2
    meta_ref[4] = lax.rem(mine, 2)

    def one_band(band, carry):
        def one_group(g, held):
            places, start = held
            size = count_ref[band, g]
            place, places = next_place(places, size)
            place_ref[band, g] = place
            own = (band == my_band) & ((place == chip) | (place == GROUPS - 1 - chip))

            @pl.when(own)
            def _():
                large = (place < HALF).astype(jnp.int32)
                meta_ref[large] = size
                base = jnp.where(large == 1, SLOTS - size, 0)
                scale = jnp.where(
                    size == 4,
                    1.0 / (4 * TIME),
                    jnp.where(size == 3, 1.0 / (3 * TIME), jnp.where(size == 2, 1.0 / (2 * TIME), 1.0 / TIME)),
                )

                def one_channel(i, carry):
                    weight_ref[base + i] = gain_ref[level_ref[band, start + i]] * scale
                    return carry

                lax.fori_loop(0, size, one_channel, 0)

            return places, start + size

        lax.fori_loop(0, GROUPS, one_group, (first_places(count_ref, band), jnp.int32(0)))
        return carry

    lax.fori_loop(0, BANDS, one_band, 0)

    def one_slot(s, carry):
        slot_ref[order_ref[s]] = s
        return carry

    lax.fori_loop(0, GROUPS, one_slot, 0, unroll=8)


def add_products(total, u_ref, v_ref, weight, imaginary):
    stations = u_ref.shape[1]
    tall = SUPER // stations
    for row in range(0, SP, SUPER):
        r = row // stations
        u = u_ref[r : r + tall].reshape(SUPER, TIME)
        v = v_ref[r : r + tall].reshape(SUPER, TIME)
        right = u_ref[r:].reshape(SP - row, TIME), v_ref[r:].reshape(SP - row, TIME)
        total[row : row + SUPER, row:] += weight * lax.dot_general(
            jnp.concatenate((v, -u) if imaginary else (u, v), 1),
            jnp.concatenate(right, 1),
            (((1,), (1,)), ((), ())),
            preferred_element_type=jnp.float32,
        )


def add_pair(core, owner, meta_ref, weight_ref, got_ref, totals):
    def one_slot(j, carry):
        t = 2 * owner + j
        large = t >= SLOTS - meta_ref[1]
        used = large | (t < meta_ref[0])
        total = totals.at[large.astype(jnp.int32)]
        for imaginary in range(2):

            @pl.when(used & (core == imaginary))
            def _():
                add_products(total, got_ref.at[:, 2 * j], got_ref.at[:, 2 * j + 1], weight_ref[t], imaginary)

        return carry

    lax.fori_loop(0, 2, one_slot, 0)


def early_kernel(meta_ref, weight_ref, mine_ref, totals):
    core = meta_ref[4]
    totals[...] = jnp.zeros_like(totals)
    add_pair(core, core, meta_ref, weight_ref, mine_ref, totals)


def visibility_kernel(meta_ref, weight_ref, slot_ref, mine_ref, other_ref, _, out_ref, totals):
    core = meta_ref[4]
    sign = (1 - 2 * core).astype(jnp.float32)
    add_pair(core, 1 - core, meta_ref, weight_ref, other_ref, totals)
    last = SLOTS - 1
    parts = mine_ref.at[:, last], other_ref.at[:, last]
    for imaginary in range(2):

        @pl.when(core == imaginary)
        def _():
            real, imag = parts[::-1] if imaginary else parts
            add_products(totals.at[1], real, imag, weight_ref[last], imaginary)

    for large in range(2):
        total = totals.at[large]

        def store(p, q, block):
            out_ref[slot_ref[SIDE * p + q], :, large] = block.reshape(BANDS, ROWS, BB)

        per = SUPER // BB
        for p in range(SIDE):
            for q in range(p // per * per, SIDE):
                block = total[p * BB : (p + 1) * BB, q * BB : (q + 1) * BB]
                store(p, q, block.astype(jnp.bfloat16))
                if q // per > p // per:
                    store(q, p, (sign * block).astype(jnp.bfloat16).T)


def place_kernel(place_ref, got_ref, out_ref, landed):
    for band in range(BANDS):

        def one_group(g, carry):
            place = place_ref[band, g]
            large = (place < HALF).astype(jnp.int32)
            chip = jnp.where(place < HALF, place, GROUPS - 1 - place)
            pltpu.make_async_copy(got_ref.at[chip, :, band, large], out_ref.at[g, band], landed).start()
            return carry

        lax.fori_loop(0, GROUPS, one_group, 0, unroll=8)
    pltpu.make_async_copy(out_ref, out_ref, landed).wait()


def body(voltages, group_count, levels, bandpass, block_order):
    stations, samples = voltages.shape[2], voltages.shape[3]
    owners = lax.axis_size("stn")
    sending = pl.pallas_call(
        build_kernel,
        out_shape=jax.ShapeDtypeStruct((owners, SLOTS, stations, samples), jnp.bfloat16),
        in_specs=[ANY, ANY],
        out_specs=ANY,
        scratch_shapes=[
            pltpu.SMEM(group_count.shape, group_count.dtype),
            pltpu.VMEM(voltages.shape, voltages.dtype),
            pltpu.SemaphoreType.DMA((2,)),
            pltpu.SemaphoreType.DMA,
        ],
        cost_estimate=pl.CostEstimate(flops=0, bytes_accessed=5 << 20, transcendentals=0),
        name="build",
    )(group_count, voltages)
    meta, weights, slots, places = pl.pallas_call(
        index_kernel,
        out_shape=(
            jax.ShapeDtypeStruct((8,), jnp.int32),
            jax.ShapeDtypeStruct((8,), jnp.float32),
            jax.ShapeDtypeStruct((GROUPS,), jnp.int32),
            jax.ShapeDtypeStruct((BANDS, GROUPS), jnp.int32),
        ),
        in_specs=[SMEM] * 4,
        out_specs=(SMEM,) * 4,
        cost_estimate=pl.CostEstimate(flops=0, bytes_accessed=8 << 20, transcendentals=0),
        compiler_params=pltpu.CompilerParams(vmem_limit_bytes=2 << 20),
        name="index",
    )(group_count, levels, bandpass, block_order)
    mine = lax.all_to_all(sending, "stn", split_axis=0, concat_axis=0, tiled=True)
    other = lax.ppermute(mine, "stn", [(i, i ^ 1) for i in range(owners)])
    totals = pl.pallas_call(
        early_kernel,
        out_shape=jax.ShapeDtypeStruct((2, SP, SP), jnp.float32),
        in_specs=[SMEM, SMEM, VMEM],
        out_specs=VMEM,
        cost_estimate=pl.CostEstimate(flops=2 << 30, bytes_accessed=10 << 20, transcendentals=0),
        compiler_params=pltpu.CompilerParams(vmem_limit_bytes=24 << 20),
        name="early",
    )(meta, weights, mine)
    blocks, _ = pl.pallas_call(
        visibility_kernel,
        out_shape=(
            jax.ShapeDtypeStruct((GROUPS, BANDS, 2, ROWS, BB), jnp.bfloat16),
            jax.ShapeDtypeStruct(totals.shape, totals.dtype),
        ),
        in_specs=[SMEM, SMEM, SMEM, VMEM, VMEM, VMEM],
        out_specs=(VMEM, VMEM),
        input_output_aliases={5: 1},
        cost_estimate=pl.CostEstimate(flops=4 << 30, bytes_accessed=9 << 20, transcendentals=0),
        compiler_params=pltpu.CompilerParams(vmem_limit_bytes=24 << 20),
        name="visibility",
    )(meta, weights, slots, mine, other, totals)
    blocks = blocks.reshape(GROUPS * BANDS, 2, ROWS, BB)
    got = lax.all_to_all(blocks, ("stn", "band"), split_axis=0, concat_axis=0, tiled=True)
    got = got.reshape(CHIPS, 2, BANDS, 2, ROWS, BB)
    out = pl.pallas_call(
        place_kernel,
        out_shape=jax.ShapeDtypeStruct((GROUPS, BANDS, 2, ROWS, BB), jnp.bfloat16),
        in_specs=[SMEM, VMEM],
        out_specs=ANY,
        scratch_shapes=[pltpu.SemaphoreType.DMA],
        cost_estimate=pl.CostEstimate(flops=0, bytes_accessed=8 << 20, transcendentals=0),
        compiler_params=pltpu.CompilerParams(vmem_limit_bytes=8 << 20),
        name="place",
    )(places, got)
    return out.reshape(1, GROUPS, BANDS, 2, ROWS, BB)


def solution(mesh):
    return jax.shard_map(
        body,
        mesh=mesh,
        in_specs=(P(None, "band", "stn", None), P(), P(), P(), P()),
        out_specs=P("stn", None, None, None, "band", None),
        check_vma=False,
    )
```

```python
import functools

import jax
import jax.numpy as jnp
from jax import lax
from jax.experimental import pallas as pl
from jax.experimental.pallas import tpu as pltpu
from jax.sharding import PartitionSpec as P


SP = 1024
TIME = 256
BB = 128
MOST = 4
GROUPS = 64
BANDS = 4
HALF = GROUPS // 2
CHIPS = 32
SLOTS = MOST + 1
SIDE = SP // BB
SUPER = 256
ROWS = BB // BANDS

SMEM = pl.BlockSpec(memory_space=pltpu.SMEM)
VMEM = pl.BlockSpec(memory_space=pltpu.VMEM)
ANY = pl.BlockSpec(memory_space=pl.ANY)


def first_places(count_ref, band):
    def tally(g, held):
        size = count_ref[band, g]
        return tuple(n + (size >= s).astype(jnp.int32) for n, s in zip(held, (4, 3, 2)))

    zero = jnp.int32(0)
    return zero, *lax.fori_loop(0, GROUPS, tally, (zero, zero, zero), unroll=True)


def next_place(places, size):
    at = [size == s for s in (4, 3, 2, 1)]
    place = jnp.where(at[0], places[0], jnp.where(at[1], places[1], jnp.where(at[2], places[2], places[3])))
    return place, tuple(p + a.astype(jnp.int32) for p, a in zip(places, at))


def build_kernel(count_ref, volt_ref, send_ref, count, held, arrivals, sent):
    band = lax.axis_index("band")
    count_copy = pltpu.make_async_copy(count_ref, count, arrivals.at[0])
    volt_copy = pltpu.make_async_copy(volt_ref, held, arrivals.at[1])
    count_copy.start()
    volt_copy.start()
    count_copy.wait()
    places = first_places(count, band)
    volt_copy.wait()

    def one_group(g, carry):
        places, start = carry
        size = count[band, g]
        place, places = next_place(places, size)
        large = place < HALF
        chip = jnp.where(large, place, GROUPS - 1 - place)
        base = jnp.where(large, SLOTS - size, 0)

        def send(i):
            target = send_ref.at[chip, pl.ds(2 * (base + i), 2)]
            pltpu.make_async_copy(held.at[:, start + i], target, sent).start()

        send(0)
        for i in range(1, MOST):
            pl.when(i < size)(functools.partial(send, i))
        return places, start + size

    lax.fori_loop(0, GROUPS, one_group, (places, jnp.int32(0)), unroll=4)
    pltpu.make_async_copy(held, held, sent).wait()


def index_kernel(count_ref, level_ref, gain_ref, order_ref, meta_ref, weight_ref, slot_ref, place_ref):
    mine = lax.axis_index("stn")
    my_band = lax.axis_index("band")
    chip = mine // 2
    meta_ref[4] = lax.rem(mine, 2)

    def one_band(band, carry):
        def one_group(g, held):
            places, start = held
            size = count_ref[band, g]
            place, places = next_place(places, size)
            place_ref[band, g] = place
            own = (band == my_band) & ((place == chip) | (place == GROUPS - 1 - chip))

            @pl.when(own)
            def _():
                large = (place < HALF).astype(jnp.int32)
                meta_ref[large] = size
                base = jnp.where(large == 1, SLOTS - size, 0)
                scale = jnp.where(
                    size == 4,
                    1.0 / (4 * TIME),
                    jnp.where(size == 3, 1.0 / (3 * TIME), jnp.where(size == 2, 1.0 / (2 * TIME), 1.0 / TIME)),
                )

                def one_channel(i, carry):
                    weight_ref[base + i] = gain_ref[level_ref[band, start + i]] * scale
                    return carry

                lax.fori_loop(0, size, one_channel, 0)

            return places, start + size

        lax.fori_loop(0, GROUPS, one_group, (first_places(count_ref, band), jnp.int32(0)))
        return carry

    lax.fori_loop(0, BANDS, one_band, 0)

    def one_slot(s, carry):
        slot_ref[order_ref[s]] = s
        return carry

    lax.fori_loop(0, GROUPS, one_slot, 0, unroll=8)


def add_products(total, u_ref, v_ref, weight, imaginary):
    stations = u_ref.shape[1]
    tall = SUPER // stations
    for row in range(0, SP, SUPER):
        r = row // stations
        u = u_ref[r : r + tall].reshape(SUPER, TIME)
        v = v_ref[r : r + tall].reshape(SUPER, TIME)
        right = u_ref[r:].reshape(SP - row, TIME), v_ref[r:].reshape(SP - row, TIME)
        total[row : row + SUPER, row:] += weight * lax.dot_general(
            jnp.concatenate((v, -u) if imaginary else (u, v), 1),
            jnp.concatenate(right, 1),
            (((1,), (1,)), ((), ())),
            preferred_element_type=jnp.float32,
        )


def add_pair(core, owner, meta_ref, weight_ref, got_ref, totals):
    def one_slot(j, carry):
        t = 3 * owner + j
        unit = owner + 2 * j
        large = t >= SLOTS - meta_ref[1]
        used = large | (t < meta_ref[0])
        total = totals.at[large.astype(jnp.int32)]
        for imaginary in range(2):

            @pl.when(used & (core == imaginary))
            def _():
                add_products(total, got_ref.at[:, unit], got_ref.at[:, unit + 1], weight_ref[t], imaginary)

        return carry

    lax.fori_loop(0, 2, one_slot, 0)


def early_kernel(meta_ref, weight_ref, mine_ref, totals):
    core = meta_ref[4]
    totals[...] = jnp.zeros_like(totals)
    add_pair(core, core, meta_ref, weight_ref, mine_ref, totals)


def visibility_kernel(meta_ref, weight_ref, slot_ref, mine_ref, other_ref, _, out_ref, totals):
    core = meta_ref[4]
    sign = (1 - 2 * core).astype(jnp.float32)
    add_pair(core, 1 - core, meta_ref, weight_ref, other_ref, totals)
    shared = 2
    for imaginary in range(2):

        @pl.when((core == imaginary) & (shared >= SLOTS - meta_ref[1]))
        def _():
            first_ref, second_ref = (other_ref, mine_ref) if imaginary else (mine_ref, other_ref)
            add_products(
                totals.at[1], first_ref.at[:, SLOTS - 1], second_ref.at[:, 0], weight_ref[shared], imaginary
            )

    for large in range(2):
        total = totals.at[large]

        def store(p, q, block):
            out_ref[slot_ref[SIDE * p + q], :, large] = block.reshape(BANDS, ROWS, BB)

        per = SUPER // BB
        for p in range(SIDE):
            for q in range(p // per * per, SIDE):
                block = total[p * BB : (p + 1) * BB, q * BB : (q + 1) * BB]
                store(p, q, block.astype(jnp.bfloat16))
                if q // per > p // per:
                    store(q, p, (sign * block).astype(jnp.bfloat16).T)


def place_kernel(place_ref, got_ref, out_ref, landed):
    for band in range(BANDS):

        def one_group(g, carry):
            place = place_ref[band, g]
            large = (place < HALF).astype(jnp.int32)
            chip = jnp.where(place < HALF, place, GROUPS - 1 - place)
            pltpu.make_async_copy(got_ref.at[chip, :, band, large], out_ref.at[g, band], landed).start()
            return carry

        lax.fori_loop(0, GROUPS, one_group, 0, unroll=8)
    pltpu.make_async_copy(out_ref, out_ref, landed).wait()


def body(voltages, group_count, levels, bandpass, block_order):
    stations, samples = voltages.shape[2], voltages.shape[3]
    owners = lax.axis_size("stn")
    sending = pl.pallas_call(
        build_kernel,
        out_shape=jax.ShapeDtypeStruct((CHIPS, 2 * SLOTS, stations, samples), jnp.bfloat16),
        in_specs=[ANY, ANY],
        out_specs=ANY,
        scratch_shapes=[
            pltpu.SMEM(group_count.shape, group_count.dtype),
            pltpu.VMEM(voltages.shape, voltages.dtype),
            pltpu.SemaphoreType.DMA((2,)),
            pltpu.SemaphoreType.DMA,
        ],
        cost_estimate=pl.CostEstimate(flops=0, bytes_accessed=5 << 20, transcendentals=0),
        name="build",
    )(group_count, voltages)
    meta, weights, slots, places = pl.pallas_call(
        index_kernel,
        out_shape=(
            jax.ShapeDtypeStruct((8,), jnp.int32),
            jax.ShapeDtypeStruct((8,), jnp.float32),
            jax.ShapeDtypeStruct((GROUPS,), jnp.int32),
            jax.ShapeDtypeStruct((BANDS, GROUPS), jnp.int32),
        ),
        in_specs=[SMEM] * 4,
        out_specs=(SMEM,) * 4,
        cost_estimate=pl.CostEstimate(flops=0, bytes_accessed=8 << 20, transcendentals=0),
        compiler_params=pltpu.CompilerParams(vmem_limit_bytes=2 << 20),
        name="index",
    )(group_count, levels, bandpass, block_order)
    sending = sending.reshape(owners, SLOTS, stations, samples)
    mine = lax.all_to_all(sending, "stn", split_axis=0, concat_axis=0, tiled=True)
    other = lax.ppermute(mine, "stn", [(i, i ^ 1) for i in range(owners)])
    totals = pl.pallas_call(
        early_kernel,
        out_shape=jax.ShapeDtypeStruct((2, SP, SP), jnp.float32),
        in_specs=[SMEM, SMEM, VMEM],
        out_specs=VMEM,
        cost_estimate=pl.CostEstimate(flops=2 << 30, bytes_accessed=10 << 20, transcendentals=0),
        compiler_params=pltpu.CompilerParams(vmem_limit_bytes=24 << 20),
        name="early",
    )(meta, weights, mine)
    blocks, _ = pl.pallas_call(
        visibility_kernel,
        out_shape=(
            jax.ShapeDtypeStruct((GROUPS, BANDS, 2, ROWS, BB), jnp.bfloat16),
            jax.ShapeDtypeStruct(totals.shape, totals.dtype),
        ),
        in_specs=[SMEM, SMEM, SMEM, VMEM, VMEM, VMEM],
        out_specs=(VMEM, VMEM),
        input_output_aliases={5: 1},
        cost_estimate=pl.CostEstimate(flops=4 << 30, bytes_accessed=9 << 20, transcendentals=0),
        compiler_params=pltpu.CompilerParams(vmem_limit_bytes=24 << 20),
        name="visibility",
    )(meta, weights, slots, mine, other, totals)
    blocks = blocks.reshape(GROUPS * BANDS, 2, ROWS, BB)
    got = lax.all_to_all(blocks, ("stn", "band"), split_axis=0, concat_axis=0, tiled=True)
    got = got.reshape(CHIPS, 2, BANDS, 2, ROWS, BB)
    out = pl.pallas_call(
        place_kernel,
        out_shape=jax.ShapeDtypeStruct((GROUPS, BANDS, 2, ROWS, BB), jnp.bfloat16),
        in_specs=[SMEM, VMEM],
        out_specs=ANY,
        scratch_shapes=[pltpu.SemaphoreType.DMA],
        cost_estimate=pl.CostEstimate(flops=0, bytes_accessed=8 << 20, transcendentals=0),
        compiler_params=pltpu.CompilerParams(vmem_limit_bytes=8 << 20),
        name="place",
    )(places, got)
    return out.reshape(1, GROUPS, BANDS, 2, ROWS, BB)


def solution(mesh):
    return jax.shard_map(
        body,
        mesh=mesh,
        in_specs=(P(None, "band", "stn", None), P(), P(), P(), P()),
        out_specs=P("stn", None, None, None, "band", None),
        check_vma=False,
    )
```

```python
import functools

import jax
import jax.numpy as jnp
from jax import lax
from jax.experimental import pallas as pl
from jax.experimental.pallas import tpu as pltpu
from jax.sharding import PartitionSpec as P


SP = 1024
TIME = 256
BB = 128
MOST = 4
GROUPS = 64
BANDS = 4
HALF = GROUPS // 2
CHIPS = 32
SLOTS = MOST + 1
SIDE = SP // BB
SUPER = 256
ROWS = BB // BANDS

SMEM = pl.BlockSpec(memory_space=pltpu.SMEM)
VMEM = pl.BlockSpec(memory_space=pltpu.VMEM)
ANY = pl.BlockSpec(memory_space=pl.ANY)


def first_places(count_ref, band):
    def tally(g, held):
        size = count_ref[band, g]
        return tuple(n + (size >= s).astype(jnp.int32) for n, s in zip(held, (4, 3, 2)))

    zero = jnp.int32(0)
    return zero, *lax.fori_loop(0, GROUPS, tally, (zero, zero, zero), unroll=True)


def next_place(places, size):
    at = [size == s for s in (4, 3, 2, 1)]
    place = jnp.where(at[0], places[0], jnp.where(at[1], places[1], jnp.where(at[2], places[2], places[3])))
    return place, tuple(p + a.astype(jnp.int32) for p, a in zip(places, at))


def build_kernel(count_ref, volt_ref, send_ref, count, held, arrivals, sent):
    band = lax.axis_index("band")
    count_copy = pltpu.make_async_copy(count_ref, count, arrivals.at[0])
    volt_copy = pltpu.make_async_copy(volt_ref, held, arrivals.at[1])
    count_copy.start()
    volt_copy.start()
    count_copy.wait()
    places = first_places(count, band)
    volt_copy.wait()

    def one_group(g, carry):
        places, start = carry
        size = count[band, g]
        place, places = next_place(places, size)
        large = place < HALF
        chip = jnp.where(large, place, GROUPS - 1 - place)
        base = jnp.where(large, SLOTS - size, 0)

        def send(i):
            target = send_ref.at[chip, pl.ds(2 * (base + i), 2)]
            pltpu.make_async_copy(held.at[:, start + i], target, sent).start()

        send(0)
        for i in range(1, MOST):
            pl.when(i < size)(functools.partial(send, i))
        return places, start + size

    lax.fori_loop(0, GROUPS, one_group, (places, jnp.int32(0)), unroll=4)
    pltpu.make_async_copy(held, held, sent).wait()


def index_kernel(count_ref, level_ref, gain_ref, order_ref, meta_ref, weight_ref, slot_ref, place_ref):
    mine = lax.axis_index("stn")
    my_band = lax.axis_index("band")
    chip = mine // 2
    meta_ref[4] = lax.rem(mine, 2)

    def one_band(band, carry):
        def one_group(g, held):
            places, start = held
            size = count_ref[band, g]
            place, places = next_place(places, size)
            place_ref[band, g] = place
            own = (band == my_band) & ((place == chip) | (place == GROUPS - 1 - chip))

            @pl.when(own)
            def _():
                large = (place < HALF).astype(jnp.int32)
                meta_ref[large] = size
                base = jnp.where(large == 1, SLOTS - size, 0)
                scale = jnp.where(
                    size == 4,
                    1.0 / (4 * TIME),
                    jnp.where(size == 3, 1.0 / (3 * TIME), jnp.where(size == 2, 1.0 / (2 * TIME), 1.0 / TIME)),
                )

                def one_channel(i, carry):
                    weight_ref[base + i] = gain_ref[level_ref[band, start + i]] * scale
                    return carry

                lax.fori_loop(0, size, one_channel, 0)

            return places, start + size

        lax.fori_loop(0, GROUPS, one_group, (first_places(count_ref, band), jnp.int32(0)))
        return carry

    lax.fori_loop(0, BANDS, one_band, 0)

    def one_slot(s, carry):
        slot_ref[order_ref[s]] = s
        return carry

    lax.fori_loop(0, GROUPS, one_slot, 0, unroll=8)


def add_products(total, u_ref, v_ref, weight, imaginary):
    stations = u_ref.shape[1]
    tall = SUPER // stations
    for row in range(0, SP, SUPER):
        r = row // stations
        u = u_ref[r : r + tall].reshape(SUPER, TIME)
        v = v_ref[r : r + tall].reshape(SUPER, TIME)
        right = u_ref[r:].reshape(SP - row, TIME), v_ref[r:].reshape(SP - row, TIME)
        total[row : row + SUPER, row:] += weight * lax.dot_general(
            jnp.concatenate((v, -u) if imaginary else (u, v), 1),
            jnp.concatenate(right, 1),
            (((1,), (1,)), ((), ())),
            preferred_element_type=jnp.float32,
        )


def add_pair(core, owner, meta_ref, weight_ref, got_ref, totals):
    def one_slot(j, carry):
        t = 3 * owner + j
        unit = owner + 2 * j
        large = t >= SLOTS - meta_ref[1]
        used = large | (t < meta_ref[0])
        total = totals.at[large.astype(jnp.int32)]
        for imaginary in range(2):

            @pl.when(used & (core == imaginary))
            def _():
                add_products(total, got_ref.at[:, unit], got_ref.at[:, unit + 1], weight_ref[t], imaginary)

        return carry

    lax.fori_loop(0, 2, one_slot, 0)


def early_kernel(meta_ref, weight_ref, mine_ref, totals):
    core = meta_ref[4]
    totals[...] = jnp.zeros_like(totals)
    add_pair(core, core, meta_ref, weight_ref, mine_ref, totals)


def visibility_kernel(meta_ref, weight_ref, slot_ref, mine_ref, other_ref, _, out_ref, totals):
    core = meta_ref[4]
    sign = (1 - 2 * core).astype(jnp.float32)
    add_pair(core, 1 - core, meta_ref, weight_ref, other_ref, totals)

    def finish(large, sign):
        total = totals.at[large]

        def store(p, q, block):
            out_ref[slot_ref[SIDE * p + q], :, large] = block.reshape(BANDS, ROWS, BB)

        per = SUPER // BB
        for p in range(SIDE):
            for q in range(p // per * per, SIDE):
                block = total[p * BB : (p + 1) * BB, q * BB : (q + 1) * BB]
                store(p, q, block.astype(jnp.bfloat16))
                if q // per > p // per:
                    store(q, p, (sign * block).astype(jnp.bfloat16).T)

    shared = 2
    held = shared >= SLOTS - meta_ref[1]
    for imaginary in range(2):

        @pl.when((core == imaginary) & held)
        def _():
            first_ref, second_ref = (other_ref, mine_ref) if imaginary else (mine_ref, other_ref)
            add_products(
                totals.at[1], first_ref.at[:, SLOTS - 1], second_ref.at[:, 0], weight_ref[shared], imaginary
            )
            finish(0, -1.0 if imaginary else 1.0)

    @pl.when(jnp.logical_not(held))
    def _():
        finish(0, sign)

    finish(1, sign)


def place_kernel(place_ref, got_ref, out_ref, landed):
    def one_group(g, carry):
        for band in range(BANDS):
            place = place_ref[band, g]
            large = (place < HALF).astype(jnp.int32)
            chip = jnp.where(place < HALF, place, GROUPS - 1 - place)
            pltpu.make_async_copy(got_ref.at[chip, :, band, large], out_ref.at[g, band], landed).start()
        return carry

    lax.fori_loop(0, GROUPS, one_group, 0, unroll=4)
    pltpu.make_async_copy(out_ref, out_ref, landed).wait()


def body(voltages, group_count, levels, bandpass, block_order):
    stations, samples = voltages.shape[2], voltages.shape[3]
    owners = lax.axis_size("stn")
    sending = pl.pallas_call(
        build_kernel,
        out_shape=jax.ShapeDtypeStruct((CHIPS, 2 * SLOTS, stations, samples), jnp.bfloat16),
        in_specs=[ANY, ANY],
        out_specs=ANY,
        scratch_shapes=[
            pltpu.SMEM(group_count.shape, group_count.dtype),
            pltpu.VMEM(voltages.shape, voltages.dtype),
            pltpu.SemaphoreType.DMA((2,)),
            pltpu.SemaphoreType.DMA,
        ],
        cost_estimate=pl.CostEstimate(flops=0, bytes_accessed=5 << 20, transcendentals=0),
        name="build",
    )(group_count, voltages)
    meta, weights, slots, places = pl.pallas_call(
        index_kernel,
        out_shape=(
            jax.ShapeDtypeStruct((8,), jnp.int32),
            jax.ShapeDtypeStruct((8,), jnp.float32),
            jax.ShapeDtypeStruct((GROUPS,), jnp.int32),
            jax.ShapeDtypeStruct((BANDS, GROUPS), jnp.int32),
        ),
        in_specs=[SMEM] * 4,
        out_specs=(SMEM,) * 4,
        cost_estimate=pl.CostEstimate(flops=0, bytes_accessed=8 << 20, transcendentals=0),
        compiler_params=pltpu.CompilerParams(vmem_limit_bytes=2 << 20),
        name="index",
    )(group_count, levels, bandpass, block_order)
    sending = sending.reshape(owners, SLOTS, stations, samples)
    mine = lax.all_to_all(sending, "stn", split_axis=0, concat_axis=0, tiled=True)
    other = lax.ppermute(mine, "stn", [(i, i ^ 1) for i in range(owners)])
    totals = pl.pallas_call(
        early_kernel,
        out_shape=jax.ShapeDtypeStruct((2, SP, SP), jnp.float32),
        in_specs=[SMEM, SMEM, VMEM],
        out_specs=VMEM,
        cost_estimate=pl.CostEstimate(flops=2 << 30, bytes_accessed=10 << 20, transcendentals=0),
        compiler_params=pltpu.CompilerParams(vmem_limit_bytes=24 << 20),
        name="early",
    )(meta, weights, mine)
    blocks, _ = pl.pallas_call(
        visibility_kernel,
        out_shape=(
            jax.ShapeDtypeStruct((GROUPS, BANDS, 2, ROWS, BB), jnp.bfloat16),
            jax.ShapeDtypeStruct(totals.shape, totals.dtype),
        ),
        in_specs=[SMEM, SMEM, SMEM, VMEM, VMEM, VMEM],
        out_specs=(VMEM, VMEM),
        input_output_aliases={5: 1},
        cost_estimate=pl.CostEstimate(flops=4 << 30, bytes_accessed=9 << 20, transcendentals=0),
        compiler_params=pltpu.CompilerParams(vmem_limit_bytes=24 << 20),
        name="visibility",
    )(meta, weights, slots, mine, other, totals)
    blocks = blocks.reshape(GROUPS * BANDS, 2, ROWS, BB)
    got = lax.all_to_all(blocks, ("stn", "band"), split_axis=0, concat_axis=0, tiled=True)
    got = got.reshape(CHIPS, 2, BANDS, 2, ROWS, BB)
    out = pl.pallas_call(
        place_kernel,
        out_shape=jax.ShapeDtypeStruct((GROUPS, BANDS, 2, ROWS, BB), jnp.bfloat16),
        in_specs=[SMEM, VMEM],
        out_specs=ANY,
        scratch_shapes=[pltpu.SemaphoreType.DMA],
        cost_estimate=pl.CostEstimate(flops=0, bytes_accessed=8 << 20, transcendentals=0),
        compiler_params=pltpu.CompilerParams(vmem_limit_bytes=8 << 20),
        name="place",
    )(places, got)
    return out.reshape(1, GROUPS, BANDS, 2, ROWS, BB)


def solution(mesh):
    return jax.shard_map(
        body,
        mesh=mesh,
        in_specs=(P(None, "band", "stn", None), P(), P(), P(), P()),
        out_specs=P("stn", None, None, None, "band", None),
        check_vma=False,
    )
```

```python
import functools

import jax
import jax.numpy as jnp
from jax import lax
from jax.experimental import pallas as pl
from jax.experimental.pallas import tpu as pltpu
from jax.sharding import PartitionSpec as P


SP = 1024
TIME = 256
BB = 128
MOST = 4
GROUPS = 64
BANDS = 4
HALF = GROUPS // 2
CHIPS = 32
SLOTS = MOST + 1
SIDE = SP // BB
SUPER = 256
ROWS = BB // BANDS

SMEM = pl.BlockSpec(memory_space=pltpu.SMEM)
VMEM = pl.BlockSpec(memory_space=pltpu.VMEM)
ANY = pl.BlockSpec(memory_space=pl.ANY)


def first_places(count_ref, band):
    def tally(g, held):
        size = count_ref[band, g]
        return tuple(n + (size >= s).astype(jnp.int32) for n, s in zip(held, (4, 3, 2)))

    zero = jnp.int32(0)
    return zero, *lax.fori_loop(0, GROUPS, tally, (zero, zero, zero), unroll=True)


def next_place(places, size):
    at = [size == s for s in (4, 3, 2, 1)]
    place = jnp.where(at[0], places[0], jnp.where(at[1], places[1], jnp.where(at[2], places[2], places[3])))
    return place, tuple(p + a.astype(jnp.int32) for p, a in zip(places, at))


def build_kernel(count_ref, volt_ref, send_ref, count, held, arrivals, sent):
    band = lax.axis_index("band")
    count_copy = pltpu.make_async_copy(count_ref, count, arrivals.at[0])
    volt_copy = pltpu.make_async_copy(volt_ref, held, arrivals.at[1])
    count_copy.start()
    volt_copy.start()
    count_copy.wait()
    places = first_places(count, band)
    volt_copy.wait()

    def one_group(g, carry):
        places, start = carry
        size = count[band, g]
        place, places = next_place(places, size)
        large = place < HALF
        chip = jnp.where(large, place, GROUPS - 1 - place)
        base = jnp.where(large, SLOTS - size, 0)

        def send(i):
            target = send_ref.at[chip, pl.ds(2 * (base + i), 2)]
            pltpu.make_async_copy(held.at[:, start + i], target, sent).start()

        send(0)
        for i in range(1, MOST):
            pl.when(i < size)(functools.partial(send, i))
        return places, start + size

    lax.fori_loop(0, GROUPS, one_group, (places, jnp.int32(0)), unroll=4)
    pltpu.make_async_copy(held, held, sent).wait()


def index_kernel(count_ref, level_ref, gain_ref, order_ref, meta_ref, weight_ref, slot_ref, place_ref):
    mine = lax.axis_index("stn")
    my_band = lax.axis_index("band")
    chip = mine // 2
    meta_ref[4] = lax.rem(mine, 2)

    def one_band(band, carry):
        def one_group(g, held):
            places, start = held
            size = count_ref[band, g]
            place, places = next_place(places, size)
            place_ref[band, g] = place
            own = (band == my_band) & ((place == chip) | (place == GROUPS - 1 - chip))

            @pl.when(own)
            def _():
                large = (place < HALF).astype(jnp.int32)
                meta_ref[large] = size
                base = jnp.where(large == 1, SLOTS - size, 0)
                scale = jnp.where(
                    size == 4,
                    1.0 / (4 * TIME),
                    jnp.where(size == 3, 1.0 / (3 * TIME), jnp.where(size == 2, 1.0 / (2 * TIME), 1.0 / TIME)),
                )

                def one_channel(i, carry):
                    weight_ref[base + i] = gain_ref[level_ref[band, start + i]] * scale
                    return carry

                lax.fori_loop(0, size, one_channel, 0)

            return places, start + size

        lax.fori_loop(0, GROUPS, one_group, (first_places(count_ref, band), jnp.int32(0)))
        return carry

    lax.fori_loop(0, BANDS, one_band, 0)

    def one_slot(s, carry):
        slot_ref[order_ref[s]] = s
        return carry

    lax.fori_loop(0, GROUPS, one_slot, 0, unroll=8)


def add_products(total, u_ref, v_ref, weight, imaginary):
    stations = u_ref.shape[1]
    tall = SUPER // stations
    for row in range(0, SP, SUPER):
        r = row // stations
        u = u_ref[r : r + tall].reshape(SUPER, TIME)
        v = v_ref[r : r + tall].reshape(SUPER, TIME)
        right = u_ref[r:].reshape(SP - row, TIME), v_ref[r:].reshape(SP - row, TIME)
        total[row : row + SUPER, row:] += weight * lax.dot_general(
            jnp.concatenate((v, -u) if imaginary else (u, v), 1),
            jnp.concatenate(right, 1),
            (((1,), (1,)), ((), ())),
            preferred_element_type=jnp.float32,
        )


def add_pair(core, owner, meta_ref, weight_ref, got_ref, totals):
    def one_slot(j, carry):
        t = 3 * owner + j
        unit = owner + 2 * j
        large = t >= SLOTS - meta_ref[1]
        used = large | (t < meta_ref[0])
        total = totals.at[large.astype(jnp.int32)]
        for imaginary in range(2):

            @pl.when(used & (core == imaginary))
            def _():
                add_products(total, got_ref.at[:, unit], got_ref.at[:, unit + 1], weight_ref[t], imaginary)

        return carry

    lax.fori_loop(0, 2, one_slot, 0)


def early_kernel(meta_ref, weight_ref, mine_ref, totals):
    core = meta_ref[4]
    totals[...] = jnp.zeros_like(totals)
    add_pair(core, core, meta_ref, weight_ref, mine_ref, totals)


def visibility_kernel(meta_ref, weight_ref, slot_ref, mine_ref, other_ref, _, out_ref, totals):
    core = meta_ref[4]
    sign = (1 - 2 * core).astype(jnp.float32)
    add_pair(core, 1 - core, meta_ref, weight_ref, other_ref, totals)

    def finish(large, sign):
        total = totals.at[large]

        def store(p, q, block):
            out_ref[:, slot_ref[SIDE * p + q], large] = block.reshape(BANDS, ROWS, BB)

        per = SUPER // BB
        for p in range(SIDE):
            for q in range(p // per * per, SIDE):
                block = total[p * BB : (p + 1) * BB, q * BB : (q + 1) * BB]
                store(p, q, block.astype(jnp.bfloat16))
                if q // per > p // per:
                    store(q, p, (sign * block).astype(jnp.bfloat16).T)

    shared = 2
    held = shared >= SLOTS - meta_ref[1]
    for imaginary in range(2):

        @pl.when((core == imaginary) & held)
        def _():
            first_ref, second_ref = (other_ref, mine_ref) if imaginary else (mine_ref, other_ref)
            add_products(
                totals.at[1], first_ref.at[:, SLOTS - 1], second_ref.at[:, 0], weight_ref[shared], imaginary
            )
            finish(0, -1.0 if imaginary else 1.0)

    @pl.when(jnp.logical_not(held))
    def _():
        finish(0, sign)

    finish(1, sign)


def place_kernel(place_ref, got_ref, out_ref, landed):
    def one_group(g, carry):
        for band in range(BANDS):
            place = place_ref[band, g]
            large = (place < HALF).astype(jnp.int32)
            chip = jnp.where(place < HALF, place, GROUPS - 1 - place)
            pltpu.make_async_copy(got_ref.at[band, chip, :, large], out_ref.at[g, band], landed).start()
        return carry

    lax.fori_loop(0, GROUPS, one_group, 0, unroll=4)
    pltpu.make_async_copy(out_ref, out_ref, landed).wait()


def body(voltages, group_count, levels, bandpass, block_order):
    stations, samples = voltages.shape[2], voltages.shape[3]
    owners = lax.axis_size("stn")
    sending = pl.pallas_call(
        build_kernel,
        out_shape=jax.ShapeDtypeStruct((CHIPS, 2 * SLOTS, stations, samples), jnp.bfloat16),
        in_specs=[ANY, ANY],
        out_specs=ANY,
        scratch_shapes=[
            pltpu.SMEM(group_count.shape, group_count.dtype),
            pltpu.VMEM(voltages.shape, voltages.dtype),
            pltpu.SemaphoreType.DMA((2,)),
            pltpu.SemaphoreType.DMA,
        ],
        cost_estimate=pl.CostEstimate(flops=0, bytes_accessed=5 << 20, transcendentals=0),
        name="build",
    )(group_count, voltages)
    meta, weights, slots, places = pl.pallas_call(
        index_kernel,
        out_shape=(
            jax.ShapeDtypeStruct((8,), jnp.int32),
            jax.ShapeDtypeStruct((8,), jnp.float32),
            jax.ShapeDtypeStruct((GROUPS,), jnp.int32),
            jax.ShapeDtypeStruct((BANDS, GROUPS), jnp.int32),
        ),
        in_specs=[SMEM] * 4,
        out_specs=(SMEM,) * 4,
        cost_estimate=pl.CostEstimate(flops=0, bytes_accessed=8 << 20, transcendentals=0),
        compiler_params=pltpu.CompilerParams(vmem_limit_bytes=2 << 20),
        name="index",
    )(group_count, levels, bandpass, block_order)
    sending = sending.reshape(owners, SLOTS, stations, samples)
    mine = lax.all_to_all(sending, "stn", split_axis=0, concat_axis=0, tiled=True)
    other = lax.ppermute(mine, "stn", [(i, i ^ 1) for i in range(owners)])
    totals = pl.pallas_call(
        early_kernel,
        out_shape=jax.ShapeDtypeStruct((2, SP, SP), jnp.float32),
        in_specs=[SMEM, SMEM, VMEM],
        out_specs=VMEM,
        cost_estimate=pl.CostEstimate(flops=2 << 30, bytes_accessed=10 << 20, transcendentals=0),
        compiler_params=pltpu.CompilerParams(vmem_limit_bytes=24 << 20),
        name="early",
    )(meta, weights, mine)
    blocks, _ = pl.pallas_call(
        visibility_kernel,
        out_shape=(
            jax.ShapeDtypeStruct((BANDS, GROUPS, 2, ROWS, BB), jnp.bfloat16),
            jax.ShapeDtypeStruct(totals.shape, totals.dtype),
        ),
        in_specs=[SMEM, SMEM, SMEM, VMEM, VMEM, VMEM],
        out_specs=(VMEM, VMEM),
        input_output_aliases={5: 1},
        cost_estimate=pl.CostEstimate(flops=4 << 30, bytes_accessed=9 << 20, transcendentals=0),
        compiler_params=pltpu.CompilerParams(vmem_limit_bytes=24 << 20),
        name="visibility",
    )(meta, weights, slots, mine, other, totals)
    blocks = blocks.reshape(GROUPS * BANDS, 2, ROWS, BB)
    got = lax.all_to_all(blocks, ("band", "stn"), split_axis=0, concat_axis=0, tiled=True)
    got = got.reshape(BANDS, CHIPS, 2, 2, ROWS, BB)
    out = pl.pallas_call(
        place_kernel,
        out_shape=jax.ShapeDtypeStruct((GROUPS, BANDS, 2, ROWS, BB), jnp.bfloat16),
        in_specs=[SMEM, VMEM],
        out_specs=ANY,
        scratch_shapes=[pltpu.SemaphoreType.DMA],
        cost_estimate=pl.CostEstimate(flops=0, bytes_accessed=8 << 20, transcendentals=0),
        compiler_params=pltpu.CompilerParams(vmem_limit_bytes=8 << 20),
        name="place",
    )(places, got)
    return out.reshape(1, GROUPS, BANDS, 2, ROWS, BB)


def solution(mesh):
    return jax.shard_map(
        body,
        mesh=mesh,
        in_specs=(P(None, "band", "stn", None), P(), P(), P(), P()),
        out_specs=P("stn", None, None, None, "band", None),
        check_vma=False,
    )
```
